32 devices in a mesh: tm: 8 (over z, x), state: 4 (over y, core).
Axes of the slice: x: 2, y: 2, z: 4, core: 2. Of those that a mesh axis runs over, the one named last changes fastest.
Arguments:
- trans_weight: bfloat16 [8, 2048, 2048], P('tm', None, 'state'), may hold values from 6e-06 to 163000
- pattern: int32 [16, 16], replicated, may hold values 0 or 1
- boundary: int32 [8], P('tm'), may hold values 0 or 1
- log_emit: float32 [8, 2048], P('tm', 'state'), may hold values from -63 to 153
Outputs:
- quad_op: float32 [4096, 2048], P('tm', 'state')
The draws below stay inside these ranges and needn't reach their ends.
All inputs are finite; a program needn't handle non-finite values. No bound on the sum of `boundary` on one device may be relied on, other than what follows from the above.
Results may differ from the reference program's by a relative error of at most 0.0003.
Values sent between devices are 32-bit elements; how exact they have to be, the bound alone decides.
A program may use at most 64 MiB of HBM per device.

```python
import jax
import jax.numpy as jnp
from jax import lax

S = 2048
BLOCK = 128
NBLK = 16
TIME = 8
QUADS = 2


def draw_log_emit(key, part):
    key_noise = jax.random.fold_in(key, 1)
    return jnp.clip(1.5 * jax.random.normal(key_noise, (TIME, S), jnp.float32), -9.0, 9.0)


def draw_trans_weight(key, part):
    key_weight = jax.random.fold_in(key, 17)
    spread = 3.0 * jnp.clip(jax.random.normal(key_weight, (TIME, S, S), jnp.float32), -4.0, 4.0)
    return jnp.exp(spread).astype(jnp.bfloat16)


def place_ends(entries, key, smallest, largest):
    longest = entries.shape.index(max(entries.shape))
    spots = []
    for shift in (0, 1):
        where = [jax.random.randint(jax.random.fold_in(key, axis), (), 0, length) for axis, length in enumerate(entries.shape)]
        where[longest] = (where[longest] + shift) % entries.shape[longest]
        spots.append(tuple(where))
    return entries.at[spots[0]].set(smallest).at[spots[1]].set(largest)


def setup_inputs(seed: int = 0) -> dict:
    splits = jax.random.split(jax.random.key(seed), 5)
    return {
        "trans_weight": draw_trans_weight(jax.random.fold_in(splits[4], 71), 0),
        "pattern": place_ends((jax.random.randint(splits[1], (NBLK, NBLK), 0, 8) < 3).astype(jnp.int32), jax.random.fold_in(splits[1], 1), 0, 1),
        "boundary": place_ends((jax.random.randint(splits[2], (TIME,), 0, 4) < 1).astype(jnp.int32), jax.random.fold_in(splits[2], 1), 0, 1),
        "log_emit": draw_log_emit(jax.random.fold_in(splits[4], 71), 0),
    }


def step_op(weight, pattern, marker, emission):
    states = weight.shape[0]
    blocks = jnp.arange(states, dtype=jnp.int32) // BLOCK
    block_mask = pattern[blocks][:, blocks].astype(jnp.float32)
    restart = 0.0001 + 0.4999 * marker.astype(jnp.float32)
    mixture = (1.0 - restart) * (4.0 / states) * weight.astype(jnp.float32) * block_mask + restart / states
    return jnp.log(mixture) + emission[None, :]


def combine(left_log, right_log):
    row_top = jnp.max(left_log, axis=1, keepdims=True)
    col_top = jnp.max(right_log, axis=0, keepdims=True)
    lead = lax.optimization_barrier(jnp.exp(left_log - row_top).astype(jnp.bfloat16)).astype(jnp.float32)
    trail = lax.optimization_barrier(jnp.exp(right_log - col_top).astype(jnp.bfloat16)).astype(jnp.float32)
    summed = jnp.dot(lead, trail, precision=lax.Precision.HIGHEST)
    return row_top + col_top + jnp.log(summed)


def reference(trans_weight, pattern, boundary, log_emit):
    def one_quad(quad_index):
        operators = []
        for member in range(4):
            position = quad_index * 4 + member
            weight = lax.dynamic_index_in_dim(trans_weight, position, 0, False)
            marker = lax.dynamic_index_in_dim(boundary, position, 0, False)
            emission = lax.dynamic_index_in_dim(log_emit, position, 0, False)
            operators.append(step_op(weight, pattern, marker, emission))
        first_pair = combine(operators[0], operators[1])
        second_pair = combine(operators[2], operators[3])
        return combine(first_pair, second_pair)

    stacked = lax.map(one_quad, jnp.arange(QUADS, dtype=jnp.int32))
    return stacked.reshape(QUADS * S, S)
```

```python
import functools
import math

import jax
import jax.numpy as jnp
from jax import lax
from jax.experimental import pallas as pl
from jax.experimental.pallas import tpu as pltpu
from jax.sharding import PartitionSpec as P

BLOCK = 128
ROWS = 64
LEAD_SHIFT = 12
TRAIL_SHIFT = -49
MESH = pl.DeviceIdType.MESH


def kernel(
    parts, w_ref, aux_ref, out_ref, left, trail, pair, first, stage, infos,
    info_send, info_recv, x_send, x_recv, y_send, y_recv, p_send, p_recv,
    q_send, q_recv, g_send, g_recv,
):
    states, width = w_ref.shape
    blocks = states // BLOCK
    chunks = states // ROWS
    per_quarter = chunks // 4
    tm = lax.axis_index("tm")
    s = lax.axis_index("state")
    base = tm // 4 * 4
    member = tm % 4
    p = member // 2
    h = member % 2
    me = member * parts + s
    core = s + 1 - 2 * (s % 2)
    over = (s + 2) % 4
    far = (core + 2) % 4
    total = 4 * parts

    def device(p_, h_, s_):
        return (base + 2 * p_ + h_, s_)

    barrier = pltpu.get_barrier_semaphore()
    for k in range(1, total):
        peer = (me + k) % total
        pl.semaphore_signal(barrier, inc=1, device_id=(base + peer // parts, peer % parts), device_id_type=MESH)
    pl.semaphore_wait(barrier, total - 1)

    info = aux_ref.at[pl.ds(blocks, 8)]

    def info_copy(k):
        peer = (me + k) % total
        return pltpu.make_async_remote_copy(
            src_ref=info, dst_ref=infos.at[me], send_sem=info_send.at[k], recv_sem=info_recv.at[k],
            device_id=(base + peer // parts, peer % parts), device_id_type=MESH)

    for k in range(1, total):
        info_copy(k).start()
    infos[me] = aux_ref[blocks:blocks + 8, :]

    def rows_of(i):
        quarter = (i + 2) % 4
        return pl.multiple_of((quarter * per_quarter + i // 4) * ROWS, ROWS)

    def remote(ref, slot, row, send, recv, target):
        view = ref.at[slot, pl.ds(row, ROWS)] if slot is not None else ref.at[pl.ds(row, ROWS)]
        return pltpu.make_async_remote_copy(
            src_ref=view, dst_ref=view, send_sem=send, recv_sem=recv, device_id=target, device_id_type=MESH)

    def x_copy(i):
        return remote(left, s, rows_of(i), x_send.at[i], x_recv.at[i], device(p, 1 - h, s))

    def y_copy(kind, i, slot, target):
        return remote(left, slot, rows_of(i), y_send.at[kind, i], y_recv.at[kind, i], device(p, h, target))

    def pair_copy(kind, i, target):
        return remote(pair, None, rows_of(i), p_send.at[kind, i], p_recv.at[i], target)

    def g_copy(kind, g, slot, target):
        row = pl.multiple_of(g * ROWS, ROWS)
        return remote(first, slot, row, g_send.at[kind, g], g_recv.at[kind, g], device(p, h, target))

    def q_copy(i):
        quarter = (i + 2) % 4
        g = i // 4
        return pltpu.make_async_remote_copy(
            src_ref=stage.at[pl.ds(rows_of(i), ROWS)],
            dst_ref=first.at[s, pl.ds(pl.multiple_of(g * ROWS, ROWS), ROWS)],
            send_sem=q_send.at[i], recv_sem=q_recv.at[g],
            device_id=(base + quarter, s), device_id_type=MESH)

    def odds(row):
        gain = aux_ref[pl.ds(row // BLOCK, 1), :]
        return 1.0 + w_ref[pl.ds(row, ROWS), :].astype(jnp.float32) * gain

    @pl.when(h == 0)
    def _():
        def send_chunk(i, c):
            row = rows_of(i)
            left[s, pl.ds(row, ROWS), :] = odds(row)
            x_copy(i).start()
            return c
        lax.fori_loop(0, chunks, send_chunk, 0)

    @pl.when(h == 1)
    def _():
        def make_trail(i, c):
            row = rows_of(i)
            trail[pl.ds(row, ROWS), :] = odds(row).astype(jnp.bfloat16)
            return c
        lax.fori_loop(0, chunks, make_trail, 0)

    def wait_info(k):
        sender = (me + total - k) % total
        pltpu.make_async_remote_copy(
            src_ref=info, dst_ref=infos.at[sender], send_sem=info_send.at[k], recv_sem=info_recv.at[k],
            device_id=(base + sender // parts, sender % parts), device_id_type=MESH).wait_recv()

    for k in range(1, total):
        wait_info(k)
        info_copy(k).wait_send()

    def emission(m, part):
        return infos[m * parts + part, 0:1, :]

    def peak(m):
        top = emission(m, 0)
        for part in range(1, parts):
            top = jnp.maximum(top, emission(m, part))
        return jnp.max(top, axis=1, keepdims=True)

    left_peak = jnp.where(p == 0, peak(0), peak(2))
    weights = [
        jnp.exp(jnp.where(p == 0, emission(0, part), emission(2, part)) - left_peak) for part in range(parts)
    ]
    middle_peak = peak(1)
    own_emission = aux_ref[blocks:blocks + 1, :]
    col_scale = jnp.where(
        p == 0, jnp.exp(own_emission - middle_peak) * 2.0 ** LEAD_SHIFT, jnp.full_like(own_emission, 2.0 ** TRAIL_SHIFT)
    )

    def combine(i):
        row = rows_of(i)
        acc = None
        for part in range(parts):
            lead = (left[part, pl.ds(row, ROWS), :] * weights[part]).astype(jnp.bfloat16)
            term = jnp.dot(lead, trail[part * width:(part + 1) * width, :], preferred_element_type=jnp.float32)
            acc = term if acc is None else acc + term
        return acc * col_scale

    def step(t, c):
        @pl.when(h == 1)
        def _():
            @pl.when(t < chunks)
            def _():
                x_copy(t).wait_recv()
                y_copy(0, t, s, core).start()
                y_copy(1, t, s, over).start()

            @pl.when((t >= 1) & (t < chunks + 1))
            def _():
                i = t - 1
                y_copy(1, i, over, over).wait_recv()
                y_copy(2, i, over, core).start()

            @pl.when((t >= 2) & (t < chunks + 2))
            def _():
                i = t - 2
                y_copy(0, i, core, core).wait_recv()
                y_copy(2, i, far, core).wait_recv()
                value = combine(i)
                row = rows_of(i)

                @pl.when(p == 1)
                def _():
                    pair[pl.ds(row, ROWS), :] = value
                    pair_copy(0, i, device(0, 1, s)).start()
                    pair_copy(1, i, device(1, 0, s)).start()

                @pl.when((p == 0) & ((i + 2) % 4 == 1))
                def _():
                    first[s, pl.ds(pl.multiple_of(i // 4 * ROWS, ROWS), ROWS), :] = value

                @pl.when((p == 0) & ((i + 2) % 4 != 1))
                def _():
                    stage[pl.ds(row, ROWS), :] = value
                    q_copy(i).start()

        @pl.when((h == 0) & (p == 1) & (t >= 3) & (t < chunks + 3))
        def _():
            i = t - 3
            pair_copy(0, i, device(0, 0, s)).wait_recv()
            pair_copy(0, i, device(0, 0, s)).start()

        @pl.when((t >= 7) & ((t - 7) % 4 == 0) & ((t - 7) // 4 < per_quarter))
        def _():
            g = (t - 7) // 4

            @pl.when(member != 1)
            def _():
                pltpu.make_async_remote_copy(
                    src_ref=stage.at[pl.ds(0, ROWS)],
                    dst_ref=first.at[s, pl.ds(pl.multiple_of(g * ROWS, ROWS), ROWS)],
                    send_sem=q_send.at[g], recv_sem=q_recv.at[g],
                    device_id=device(0, 1, over), device_id_type=MESH).wait_recv()
            g_copy(0, g, s, core).start()
            g_copy(1, g, s, over).start()

        @pl.when((t >= 9) & ((t - 9) % 4 == 0))
        def _():
            g = (t - 9) // 4
            g_copy(1, g, over, over).wait_recv()
            g_copy(2, g, over, core).start()
        return c

    lax.fori_loop(0, chunks + 6, step, 0)

    @pl.when(p == 0)
    def _():
        def wait_pair(i, c):
            pair_copy(0, i, device(1, h, s)).wait_recv()
            return c
        lax.fori_loop(0, chunks, wait_pair, 0)

    def to_trail(i, c):
        row = pl.multiple_of(i * ROWS, ROWS)
        trail[pl.ds(row, ROWS), :] = pair[pl.ds(row, ROWS), :].astype(jnp.bfloat16)
        return c

    lax.fori_loop(0, chunks, to_trail, 0)

    def wait_gather(g, c):
        g_copy(0, g, core, core).wait_recv()
        g_copy(2, g, far, core).wait_recv()
        return c

    lax.fori_loop(0, per_quarter, wait_gather, 0)

    log_shares = infos[0, 1:2, :] + infos[parts, 1:2, :] + infos[2 * parts, 1:2, :] + infos[3 * parts, 1:2, :]
    shift = math.log(2.0) * (LEAD_SHIFT + TRAIL_SHIFT)
    last_emission = jnp.zeros_like(own_emission)
    for part in range(parts):
        last_emission = jnp.where(s == part, emission(3, part), last_emission)
    offset = last_emission + log_shares + (peak(0) + middle_peak + peak(2) - shift)

    out_rows = out_ref.shape[0]
    tile = 128

    def finish(i, c):
        row = pl.multiple_of(i * tile, tile)
        acc = None
        for part in range(parts):
            term = jnp.dot(
                first[part, pl.ds(row, tile), :].astype(jnp.bfloat16), trail[part * width:(part + 1) * width, :],
                preferred_element_type=jnp.float32)
            acc = term if acc is None else acc + term
        out_ref[pl.ds(row, tile), :] = jnp.log(acc) + offset
        return c

    lax.fori_loop(0, out_rows // tile, finish, 0)

    @pl.when(h == 0)
    def _():
        def drain(i, c):
            x_copy(i).wait_send()
            return c
        lax.fori_loop(0, chunks, drain, 0)

        @pl.when(p == 1)
        def _():
            def drain_pair(i, c):
                pair_copy(0, i, device(0, 0, s)).wait_send()
                return c
            lax.fori_loop(0, chunks, drain_pair, 0)

    @pl.when(h == 1)
    def _():
        def drain(i, c):
            y_copy(0, i, s, core).wait_send()
            y_copy(1, i, s, over).wait_send()
            y_copy(2, i, over, core).wait_send()

            @pl.when(p == 1)
            def _():
                pair_copy(0, i, device(0, 1, s)).wait_send()
                pair_copy(1, i, device(1, 0, s)).wait_send()

            @pl.when((p == 0) & ((i + 2) % 4 != 1))
            def _():
                q_copy(i).wait_send()
            return c
        lax.fori_loop(0, chunks, drain, 0)

    def drain_gather(g, c):
        g_copy(0, g, s, core).wait_send()
        g_copy(1, g, s, over).wait_send()
        g_copy(2, g, over, core).wait_send()
        return c

    lax.fori_loop(0, per_quarter, drain_gather, 0)


def on_device(parts, trans_weight, pattern, boundary, log_emit):
    weight = trans_weight[0]
    states, width = weight.shape
    blocks = pattern.shape[0]
    restart = 0.0001 + 0.4999 * boundary.astype(jnp.float32)
    first_block = lax.axis_index("state") * (width // BLOCK)
    mine = lax.dynamic_slice_in_dim(pattern, first_block, width // BLOCK, 1).astype(jnp.float32)
    gain = jnp.repeat(mine, BLOCK, axis=1) * (4.0 * (1.0 - restart) / restart)
    share = jnp.broadcast_to(jnp.log(restart / states)[:, None], (7, width))
    aux = jnp.concatenate([gain, log_emit, share], axis=0)
    chunks = states // ROWS
    dma = pltpu.SemaphoreType.DMA
    vmem = pl.BlockSpec(memory_space=pltpu.VMEM)
    return pl.pallas_call(
        functools.partial(kernel, parts),
        out_shape=jax.ShapeDtypeStruct((states // 4, width), jnp.float32),
        in_specs=[vmem, vmem],
        out_specs=vmem,
        scratch_shapes=[
            pltpu.VMEM((parts, states, width), jnp.float32),
            pltpu.VMEM((states, width), jnp.bfloat16),
            pltpu.VMEM((states, width), jnp.float32),
            pltpu.VMEM((parts, states // 4, width), jnp.float32),
            pltpu.VMEM((states, width), jnp.float32),
            pltpu.VMEM((4 * parts, 8, width), jnp.float32),
            dma((4 * parts,)), dma((4 * parts,)),
            dma((chunks,)), dma((chunks,)),
            dma((3, chunks)), dma((3, chunks)),
            dma((2, chunks)), dma((chunks,)),
            dma((chunks,)), dma((chunks // 4,)),
            dma((3, chunks // 4)), dma((3, chunks // 4)),
        ],
        compiler_params=pltpu.CompilerParams(
            collective_id=0, has_side_effects=True, vmem_limit_bytes=52 * 1024 * 1024
        ),
    )(weight, aux)


def solution(mesh):
    return jax.shard_map(
        functools.partial(on_device, mesh.shape["state"]),
        mesh=mesh,
        in_specs=(P("tm", None, "state"), P(), P("tm"), P("tm", "state")),
        out_specs=P("tm", "state"),
        check_vma=False,
    )
```

```python
import functools
import math

import jax
import jax.numpy as jnp
from jax import lax
from jax.experimental import pallas as pl
from jax.experimental.pallas import tpu as pltpu
from jax.sharding import PartitionSpec as P

BLOCK = 128
ROWS = 64
STRIPS = 4
TILE = 256
SCHEDULE = (
    (0, 16, 0, None), (16, 19, None, 0), (19, 21, 1, None), (21, 24, None, 1), (24, 26, 2, None), (26, 30, None, 2),
    (30, 32, 3, 3),
)
LEAD_SHIFT = 12
TRAIL_SHIFT = -49
MESH = pl.DeviceIdType.MESH


def kernel(
    parts, w_ref, aux_ref, out_ref, left, trail, pair, first, stage, right, infos,
    info_send, info_recv, x_send, x_recv, y_send, y_recv, p_send, p_recv,
    q_send, q_recv, g_send, g_recv, b_send, b_recv, w_send, w_recv, v_send, v_recv,
):
    states, width = w_ref.shape
    blocks = states // BLOCK
    chunks = states // ROWS
    per_quarter = chunks // 4
    half = chunks // 2
    quarter_rows = states // 4
    strip = width // STRIPS
    tm = lax.axis_index("tm")
    s = lax.axis_index("state")
    base = tm // 4 * 4
    member = tm % 4
    p = member // 2
    h = member % 2
    me = member * parts + s
    core = s + 1 - 2 * (s % 2)
    over = (s + 2) % 4
    far = (core + 2) % 4
    total = 4 * parts

    def device(p_, h_, s_):
        return (base + 2 * p_ + h_, s_)

    barrier = pltpu.get_barrier_semaphore()
    for k in range(1, total):
        peer = (me + k) % total
        pl.semaphore_signal(barrier, inc=1, device_id=(base + peer // parts, peer % parts), device_id_type=MESH)
    pl.semaphore_wait(barrier, total - 1)

    info = aux_ref.at[pl.ds(blocks, 8)]

    def info_copy(k):
        peer = (me + k) % total
        return pltpu.make_async_remote_copy(
            src_ref=info, dst_ref=infos.at[me], send_sem=info_send.at[k], recv_sem=info_recv.at[k],
            device_id=(base + peer // parts, peer % parts), device_id_type=MESH)

    for k in range(1, total):
        info_copy(k).start()
    infos[me] = aux_ref[blocks:blocks + 8, :]

    def rows_of(i):
        return pl.multiple_of(i * ROWS, ROWS)

    def remote(ref, slot, row, send, recv, target):
        view = ref.at[slot, pl.ds(row, ROWS)] if slot is not None else ref.at[pl.ds(row, ROWS)]
        return pltpu.make_async_remote_copy(
            src_ref=view, dst_ref=view, send_sem=send, recv_sem=recv, device_id=target, device_id_type=MESH)

    def half_rows(i, side):
        return pl.multiple_of(((2 + side - 2 * (i % 2)) * per_quarter + i // 2) * ROWS, ROWS)

    def x_copy(i, row):
        return remote(left, s, row, x_send.at[i], x_recv.at[i], device(p, 1 - h, s))

    def y_copy(kind, i, row, slot, target):
        return remote(left, slot, row, y_send.at[kind, i], y_recv.at[kind, i], device(p, h, target))

    def pair_copy(kind, i, target):
        return remote(pair, None, rows_of(i), p_send.at[kind, i], p_recv.at[i], target)

    def local_row(g):
        return pl.multiple_of(g * ROWS, ROWS)

    def g_copy(kind, g, slot, target):
        return remote(first, slot, local_row(g), g_send.at[kind, g], g_recv.at[kind, g], device(p, h, target))

    def columns(n):
        return pl.ds(n * strip, strip)

    def g_strip(kind, n, slot, target):
        view = first.at[slot, :, columns(n)]
        return pltpu.make_async_remote_copy(
            src_ref=view, dst_ref=view, send_sem=g_send.at[kind, n], recv_sem=g_recv.at[kind, n],
            device_id=device(p, h, target), device_id_type=MESH)

    def q_copy(g):
        return pltpu.make_async_remote_copy(
            src_ref=stage.at[pl.ds(local_row(g), ROWS)], dst_ref=first.at[s, pl.ds(local_row(g), ROWS)],
            send_sem=q_send.at[g], recv_sem=q_recv.at[g], device_id=device(1 - p, 1, s), device_id_type=MESH)

    def q_strip(n):
        return pltpu.make_async_remote_copy(
            src_ref=stage.at[pl.ds(0, quarter_rows), columns(n)], dst_ref=first.at[s, :, columns(n)],
            send_sem=q_send.at[n], recv_sem=q_recv.at[n], device_id=device(1 - p, 0, s), device_id_type=MESH)

    def w_copy(g):
        return pltpu.make_async_remote_copy(
            src_ref=stage.at[pl.ds(local_row(g), ROWS)], dst_ref=stage.at[pl.ds(local_row(g + per_quarter), ROWS)],
            send_sem=w_send.at[g], recv_sem=w_recv.at[g], device_id=device(p, h, over), device_id_type=MESH)

    def v_copy(g):
        return pltpu.make_async_remote_copy(
            src_ref=stage.at[pl.ds(local_row(g + per_quarter), ROWS)], dst_ref=first.at[over, pl.ds(local_row(g), ROWS)],
            send_sem=v_send.at[g], recv_sem=v_recv.at[g], device_id=device(1 - p, 1, s), device_id_type=MESH)

    def b_copy(n):
        view = right.at[:, columns(n)]
        return pltpu.make_async_remote_copy(
            src_ref=view, dst_ref=view, send_sem=b_send.at[n], recv_sem=b_recv.at[n],
            device_id=device(p, 1 - h, s), device_id_type=MESH)

    def odds(row):
        gain = aux_ref[pl.ds(row // BLOCK, 1), :]
        return 1.0 + w_ref[pl.ds(row, ROWS), :].astype(jnp.float32) * gain

    def loop(count, body):
        def run(i, c):
            body(i)
            return c
        lax.fori_loop(0, count, run, 0)

    @pl.when((h == 0) & (p == 1))
    def _():
        @functools.partial(loop, chunks)
        def _(i):
            row = rows_of(i)
            left[s, pl.ds(row, ROWS), :] = odds(row)
            x_copy(i, row).start()

    @pl.when((h == 0) & (p == 0))
    def _():
        @functools.partial(loop, half)
        def _(i):
            row = half_rows(i, 1)
            left[s, pl.ds(row, ROWS), :] = odds(row)
            x_copy(i, row).start()
            near = half_rows(i, 0)
            left[s, pl.ds(near, ROWS), :] = odds(near)
            y_copy(0, i, near, s, core).start()
            y_copy(1, i, near, s, over).start()

    @pl.when((h == 1) & (p == 1))
    def _():
        @functools.partial(loop, chunks)
        def _(i):
            row = local_row(i)
            trail[pl.ds(row, ROWS), :] = odds(row).astype(jnp.bfloat16)

    @pl.when((h == 1) & (p == 0))
    def _():
        for n in range(STRIPS):
            @functools.partial(loop, chunks)
            def _(i):
                row = local_row(i)
                gain = aux_ref[pl.ds(row // BLOCK, 1), :][:, n * strip:(n + 1) * strip]
                value = 1.0 + w_ref[pl.ds(row, ROWS), columns(n)].astype(jnp.float32) * gain
                right[pl.ds(row, ROWS), columns(n)] = value
                trail[pl.ds(row, ROWS), columns(n)] = value.astype(jnp.bfloat16)
            b_copy(n).start()

    def wait_info(k):
        sender = (me + total - k) % total
        pltpu.make_async_remote_copy(
            src_ref=info, dst_ref=infos.at[sender], send_sem=info_send.at[k], recv_sem=info_recv.at[k],
            device_id=(base + sender // parts, sender % parts), device_id_type=MESH).wait_recv()

    for k in range(1, total):
        wait_info(k)
        info_copy(k).wait_send()

    def emission(m, part):
        return infos[m * parts + part, 0:1, :]

    def peak(m):
        top = emission(m, 0)
        for part in range(1, parts):
            top = jnp.maximum(top, emission(m, part))
        return jnp.max(top, axis=1, keepdims=True)

    left_peak = jnp.where(p == 0, peak(0), peak(2))
    weights = [
        jnp.exp(jnp.where(p == 0, emission(0, part), emission(2, part)) - left_peak) for part in range(parts)
    ]
    middle_peak = peak(1)
    middle_emission = infos[parts + s, 0:1, :]
    middle_scale = jnp.exp(middle_emission - middle_peak) * 2.0 ** LEAD_SHIFT

    def product(row, count, n):
        acc = None
        for part in range(parts):
            lead = (left[part, pl.ds(row, count), :] * weights[part]).astype(jnp.bfloat16)
            block = slice(part * width, (part + 1) * width)
            right_block = trail[block, :] if n is None else trail[block, n * strip:(n + 1) * strip]
            term = jnp.dot(lead, right_block, preferred_element_type=jnp.float32)
            acc = term if acc is None else acc + term
        return acc

    def take(i, row):
        x_copy(i, row).wait_recv()
        y_copy(0, i, row, s, core).start()
        y_copy(1, i, row, s, over).start()

    def relay(i, row):
        y_copy(1, i, row, over, over).wait_recv()
        y_copy(2, i, row, over, core).start()

    def have(i, row):
        y_copy(0, i, row, core, core).wait_recv()
        y_copy(2, i, row, far, core).wait_recv()

    @pl.when((p == 1) & (h == 1))
    def _():
        @functools.partial(loop, chunks + 2)
        def _(t):
            @pl.when(t < chunks)
            def _():
                take(t, rows_of(t))

            @pl.when((t >= 1) & (t < chunks + 1))
            def _():
                relay(t - 1, rows_of(t - 1))

            @pl.when((t >= 3) & (t % 2 == 1))
            def _():
                i = t - 3
                row = pl.multiple_of(rows_of(i), 2 * ROWS)
                have(i, rows_of(i))
                have(i + 1, rows_of(i + 1))
                pair[pl.ds(row, 2 * ROWS), :] = product(row, 2 * ROWS, None) * 2.0 ** TRAIL_SHIFT
                pair_copy(1, i, device(1, 0, s)).start()
                pair_copy(0, i, device(0, 1, s)).start()
                pair_copy(1, i + 1, device(1, 0, s)).start()
                pair_copy(0, i + 1, device(0, 1, s)).start()

            @pl.when((t >= 11) & ((t - 11) % 2 == 0) & ((t - 11) // 2 < per_quarter))
            def _():
                g = (t - 11) // 2
                q_copy(g).wait_recv()
                g_copy(0, g, s, core).start()
                v_copy(g).wait_recv()
                g_copy(2, g, over, core).start()

    @pl.when((p == 0) & (h == 1))
    def _():
        @functools.partial(loop, half + 5)
        def _(t):
            @pl.when(t < half)
            def _():
                take(t, half_rows(t, 1))

            @pl.when((t >= 1) & (t < half + 1))
            def _():
                relay(t - 1, half_rows(t - 1, 1))

            @pl.when((t >= 2) & (t < half + 2))
            def _():
                i = t - 2
                g = i // 2
                row = half_rows(i, 1)
                have(i, row)
                value = product(row, ROWS, None) * middle_scale

                @pl.when(i % 2 == 0)
                def _():
                    stage[pl.ds(local_row(g), ROWS), :] = value
                    w_copy(g).start()
                    q_copy(g).start()

                @pl.when(i % 2 == 1)
                def _():
                    first[s, pl.ds(local_row(g), ROWS), :] = value
                    g_copy(1, g, s, over).start()
                    g_copy(0, g, s, core).start()

            @pl.when(t >= 5)
            def _():
                i = t - 5
                g = i // 2

                @pl.when(i % 2 == 0)
                def _():
                    w_copy(g).wait_recv()
                    v_copy(g).start()

                @pl.when(i % 2 == 1)
                def _():
                    g_copy(1, g, over, over).wait_recv()
                    g_copy(2, g, over, core).start()

    def strip_out(n):
        g_strip(1, n, s, over).start()
        g_strip(0, n, s, core).start()

    def strip_relay(n):
        g_strip(1, n, over, over).wait_recv()
        g_strip(2, n, over, core).start()

    @pl.when((p == 1) & (h == 0))
    def _():
        for low, high, arrive, pass_on in SCHEDULE:
            def relay_pair(i, c):
                pair_copy(0, i, device(0, 0, s)).wait_recv()
                pair_copy(0, i, device(0, 0, s)).start()
                return c
            lax.fori_loop(chunks * low // 32, chunks * high // 32, relay_pair, 0)
            if arrive is not None:
                q_strip(arrive).wait_recv()
                strip_out(arrive)
            if pass_on is not None:
                strip_relay(pass_on)

    @pl.when((p == 0) & (h == 0))
    def _():
        @functools.partial(loop, half)
        def _(i):
            relay(i, half_rows(i, 0))

        @functools.partial(loop, half)
        def _(i):
            have(i, half_rows(i, 0))

        for n in range(STRIPS):
            b_copy(n).wait_recv()

            @functools.partial(loop, chunks)
            def _(i):
                row = local_row(i)
                trail[pl.ds(row, ROWS), columns(n)] = right[pl.ds(row, ROWS), columns(n)].astype(jnp.bfloat16)

            scale = middle_scale[:, n * strip:(n + 1) * strip]

            @functools.partial(loop, quarter_rows // TILE)
            def _(j):
                row = pl.multiple_of(j * TILE, TILE)
                source = pl.multiple_of(2 * quarter_rows + j * TILE, TILE)
                stage[pl.ds(row, TILE), columns(n)] = product(source, TILE, n) * scale

            q_strip(n).start()

            @functools.partial(loop, quarter_rows // TILE)
            def _(j):
                row = pl.multiple_of(j * TILE, TILE)
                first[s, pl.ds(row, TILE), columns(n)] = product(row, TILE, n) * scale

            strip_out(n)
            if n > 0:
                strip_relay(n - 1)
        strip_relay(STRIPS - 1)

    @pl.when(p == 0)
    def _():
        @functools.partial(loop, chunks)
        def _(i):
            pair_copy(0, i, device(1, h, s)).wait_recv()

    def to_trail(i, c):
        row = pl.multiple_of(i * ROWS, ROWS)
        trail[pl.ds(row, ROWS), :] = pair[pl.ds(row, ROWS), :].astype(jnp.bfloat16)
        return c

    lax.fori_loop(0, chunks, to_trail, 0)

    @pl.when(h == 1)
    def _():
        @functools.partial(loop, per_quarter)
        def _(g):
            g_copy(0, g, core, core).wait_recv()
            g_copy(2, g, far, core).wait_recv()

    @pl.when(h == 0)
    def _():
        for n in range(STRIPS):
            g_strip(0, n, core, core).wait_recv()
            g_strip(2, n, far, core).wait_recv()

    log_shares = infos[0, 1:2, :] + infos[parts, 1:2, :] + infos[2 * parts, 1:2, :] + infos[3 * parts, 1:2, :]
    shift = math.log(2.0) * (LEAD_SHIFT + TRAIL_SHIFT)
    last_emission = jnp.zeros_like(middle_emission)
    for part in range(parts):
        last_emission = jnp.where(s == part, emission(3, part), last_emission)
    offset = last_emission + log_shares + (peak(0) + middle_peak + peak(2) - shift)

    out_rows = out_ref.shape[0]
    tile = 128

    def finish(i, c):
        row = pl.multiple_of(i * tile, tile)
        acc = None
        for part in range(parts):
            term = jnp.dot(
                first[part, pl.ds(row, tile), :].astype(jnp.bfloat16), trail[part * width:(part + 1) * width, :],
                preferred_element_type=jnp.float32)
            acc = term if acc is None else acc + term
        out_ref[pl.ds(row, tile), :] = jnp.log(acc) + offset
        return c

    lax.fori_loop(0, out_rows // tile, finish, 0)

    def drain_left(i, row):
        y_copy(0, i, row, s, core).wait_send()
        y_copy(1, i, row, s, over).wait_send()
        y_copy(2, i, row, over, core).wait_send()

    @pl.when((p == 1) & (h == 1))
    def _():
        @functools.partial(loop, chunks)
        def _(i):
            drain_left(i, rows_of(i))
            pair_copy(0, i, device(0, 1, s)).wait_send()
            pair_copy(1, i, device(1, 0, s)).wait_send()

        @functools.partial(loop, per_quarter)
        def _(g):
            g_copy(0, g, s, core).wait_send()
            g_copy(2, g, over, core).wait_send()

    @pl.when((p == 1) & (h == 0))
    def _():
        @functools.partial(loop, chunks)
        def _(i):
            x_copy(i, rows_of(i)).wait_send()
            pair_copy(0, i, device(0, 0, s)).wait_send()

    @pl.when((p == 0) & (h == 1))
    def _():
        for n in range(STRIPS):
            b_copy(n).wait_send()

        @functools.partial(loop, half)
        def _(i):
            drain_left(i, half_rows(i, 1))

        @functools.partial(loop, per_quarter)
        def _(g):
            q_copy(g).wait_send()
            w_copy(g).wait_send()
            v_copy(g).wait_send()
            g_copy(0, g, s, core).wait_send()
            g_copy(1, g, s, over).wait_send()
            g_copy(2, g, over, core).wait_send()

    @pl.when((p == 0) & (h == 0))
    def _():
        @functools.partial(loop, half)
        def _(i):
            x_copy(i, half_rows(i, 1)).wait_send()
            drain_left(i, half_rows(i, 0))

        for n in range(STRIPS):
            q_strip(n).wait_send()

    @pl.when(h == 0)
    def _():
        for n in range(STRIPS):
            g_strip(0, n, s, core).wait_send()
            g_strip(1, n, s, over).wait_send()
            g_strip(2, n, over, core).wait_send()


def on_device(parts, trans_weight, pattern, boundary, log_emit):
    weight = trans_weight[0]
    states, width = weight.shape
    blocks = pattern.shape[0]
    restart = 0.0001 + 0.4999 * boundary.astype(jnp.float32)
    first_block = lax.axis_index("state") * (width // BLOCK)
    mine = lax.dynamic_slice_in_dim(pattern, first_block, width // BLOCK, 1).astype(jnp.float32)
    gain = jnp.repeat(mine, BLOCK, axis=1) * (4.0 * (1.0 - restart) / restart)
    share = jnp.broadcast_to(jnp.log(restart / states)[:, None], (7, width))
    aux = jnp.concatenate([gain, log_emit, share], axis=0)
    chunks = states // ROWS
    dma = pltpu.SemaphoreType.DMA
    vmem = pl.BlockSpec(memory_space=pltpu.VMEM)
    return pl.pallas_call(
        functools.partial(kernel, parts),
        out_shape=jax.ShapeDtypeStruct((states // 4, width), jnp.float32),
        in_specs=[vmem, vmem],
        out_specs=vmem,
        scratch_shapes=[
            pltpu.VMEM((parts, states, width), jnp.float32),
            pltpu.VMEM((states, width), jnp.bfloat16),
            pltpu.VMEM((states, width), jnp.float32),
            pltpu.VMEM((parts, states // 4, width), jnp.float32),
            pltpu.VMEM((states, width), jnp.float32),
            pltpu.VMEM((states, width), jnp.float32),
            pltpu.VMEM((4 * parts, 8, width), jnp.float32),
            dma((4 * parts,)), dma((4 * parts,)),
            dma((chunks,)), dma((chunks,)),
            dma((3, chunks)), dma((3, chunks)),
            dma((2, chunks)), dma((chunks,)),
            dma((chunks // 4,)), dma((chunks // 4,)),
            dma((3, chunks // 4)), dma((3, chunks // 4)),
            dma((STRIPS,)), dma((STRIPS,)),
            dma((chunks // 4,)), dma((chunks // 4,)), dma((chunks // 4,)), dma((chunks // 4,)),
        ],
        compiler_params=pltpu.CompilerParams(
            collective_id=0, has_side_effects=True, vmem_limit_bytes=52 * 1024 * 1024
        ),
    )(weight, aux)


def solution(mesh):
    return jax.shard_map(
        functools.partial(on_device, mesh.shape["state"]),
        mesh=mesh,
        in_specs=(P("tm", None, "state"), P(), P("tm"), P("tm", "state")),
        out_specs=P("tm", "state"),
        check_vma=False,
    )
```

```python
import functools
import math

import jax
import jax.numpy as jnp
from jax import lax
from jax.experimental import pallas as pl
from jax.experimental.pallas import tpu as pltpu
from jax.sharding import PartitionSpec as P

BLOCK = 128
ROWS = 64
STRIPS = 4
TILE = 256
SCHEDULE = (
    (0, 16, 0, None), (16, 19, None, 0), (19, 21, 1, None), (21, 24, None, 1), (24, 26, 2, None), (26, 30, None, 2),
    (30, 32, 3, 3),
)
LEAD_SHIFT = 12
TRAIL_SHIFT = -49
MESH = pl.DeviceIdType.MESH


def kernel(
    parts, w_ref, aux_ref, out_ref, left, trail, pair, first, stage, right, infos,
    info_send, info_recv, x_send, x_recv, y_send, y_recv, p_send, p_recv,
    q_send, q_recv, g_send, g_recv, b_send, b_recv, w_send, w_recv, v_send, v_recv,
):
    states, width = w_ref.shape
    blocks = states // BLOCK
    chunks = states // ROWS
    per_quarter = chunks // 4
    half = chunks // 2
    quarter_rows = states // 4
    strip = width // STRIPS
    tm = lax.axis_index("tm")
    s = lax.axis_index("state")
    base = tm // 4 * 4
    member = tm % 4
    p = member // 2
    h = member % 2
    me = member * parts + s
    core = s + 1 - 2 * (s % 2)
    over = (s + 2) % 4
    far = (core + 2) % 4
    total = 4 * parts

    def device(p_, h_, s_):
        return (base + 2 * p_ + h_, s_)

    barrier = pltpu.get_barrier_semaphore()
    for k in range(1, total):
        peer = (me + k) % total
        pl.semaphore_signal(barrier, inc=1, device_id=(base + peer // parts, peer % parts), device_id_type=MESH)
    pl.semaphore_wait(barrier, total - 1)

    info = aux_ref.at[pl.ds(blocks, 8)]

    def info_copy(k):
        peer = (me + k) % total
        return pltpu.make_async_remote_copy(
            src_ref=info, dst_ref=infos.at[me], send_sem=info_send.at[k], recv_sem=info_recv.at[k],
            device_id=(base + peer // parts, peer % parts), device_id_type=MESH)

    for k in range(1, total):
        info_copy(k).start()
    infos[me] = aux_ref[blocks:blocks + 8, :]

    def rows_of(i):
        return pl.multiple_of(i * ROWS, ROWS)

    def remote(ref, slot, row, send, recv, target):
        view = ref.at[slot, pl.ds(row, ROWS)] if slot is not None else ref.at[pl.ds(row, ROWS)]
        return pltpu.make_async_remote_copy(
            src_ref=view, dst_ref=view, send_sem=send, recv_sem=recv, device_id=target, device_id_type=MESH)

    def half_rows(i, side):
        return pl.multiple_of(((2 + side - 2 * (i % 2)) * per_quarter + i // 2) * ROWS, ROWS)

    def x_copy(i, row):
        return remote(left, s, row, x_send.at[i], x_recv.at[i], device(p, 1 - h, s))

    def y_copy(kind, i, row, slot, target):
        return remote(left, slot, row, y_send.at[kind, i], y_recv.at[kind, i], device(p, h, target))

    def pair_copy(kind, i, target):
        return remote(pair, None, rows_of(i), p_send.at[kind, i], p_recv.at[i], target)

    def local_row(g):
        return pl.multiple_of(g * ROWS, ROWS)

    def g_copy(kind, g, slot, target):
        return remote(first, slot, local_row(g), g_send.at[kind, g], g_recv.at[kind, g], device(p, h, target))

    def columns(n):
        return pl.ds(n * strip, strip)

    def g_strip(kind, n, slot, target):
        view = first.at[slot, :, columns(n)]
        return pltpu.make_async_remote_copy(
            src_ref=view, dst_ref=view, send_sem=g_send.at[kind, n], recv_sem=g_recv.at[kind, n],
            device_id=device(p, h, target), device_id_type=MESH)

    def q_copy(g):
        return pltpu.make_async_remote_copy(
            src_ref=stage.at[pl.ds(local_row(g), ROWS)], dst_ref=first.at[s, pl.ds(local_row(g), ROWS)],
            send_sem=q_send.at[g], recv_sem=q_recv.at[g], device_id=device(1 - p, 1, s), device_id_type=MESH)

    def q_strip(n):
        return pltpu.make_async_remote_copy(
            src_ref=stage.at[pl.ds(0, quarter_rows), columns(n)], dst_ref=first.at[s, :, columns(n)],
            send_sem=q_send.at[n], recv_sem=q_recv.at[n], device_id=device(1 - p, 0, s), device_id_type=MESH)

    def w_copy(g):
        return pltpu.make_async_remote_copy(
            src_ref=stage.at[pl.ds(local_row(g), ROWS)], dst_ref=stage.at[pl.ds(local_row(g + per_quarter), ROWS)],
            send_sem=w_send.at[g], recv_sem=w_recv.at[g], device_id=device(p, h, over), device_id_type=MESH)

    def v_copy(g):
        return pltpu.make_async_remote_copy(
            src_ref=stage.at[pl.ds(local_row(g + per_quarter), ROWS)], dst_ref=first.at[over, pl.ds(local_row(g), ROWS)],
            send_sem=v_send.at[g], recv_sem=v_recv.at[g], device_id=device(1 - p, 1, s), device_id_type=MESH)

    def b_copy(n):
        view = right.at[:, columns(n)]
        return pltpu.make_async_remote_copy(
            src_ref=view, dst_ref=view, send_sem=b_send.at[n], recv_sem=b_recv.at[n],
            device_id=device(p, 1 - h, s), device_id_type=MESH)

    def odds(row):
        gain = aux_ref[pl.ds(row // BLOCK, 1), :]
        return 1.0 + w_ref[pl.ds(row, ROWS), :].astype(jnp.float32) * gain

    def loop(count, body):
        def run(i, c):
            body(i)
            return c
        lax.fori_loop(0, count, run, 0)

    @pl.when((h == 0) & (p == 1))
    def _():
        @functools.partial(loop, chunks)
        def _(i):
            row = rows_of(i)
            left[s, pl.ds(row, ROWS), :] = odds(row)
            x_copy(i, row).start()

    @pl.when((h == 0) & (p == 0))
    def _():
        @functools.partial(loop, half)
        def _(i):
            row = half_rows(i, 1)
            left[s, pl.ds(row, ROWS), :] = odds(row)
            x_copy(i, row).start()
            near = half_rows(i, 0)
            left[s, pl.ds(near, ROWS), :] = odds(near)
            y_copy(0, i, near, s, core).start()
            y_copy(1, i, near, s, over).start()

    @pl.when((h == 1) & (p == 1))
    def _():
        @functools.partial(loop, chunks)
        def _(i):
            row = local_row(i)
            trail[pl.ds(row, ROWS), :] = odds(row).astype(jnp.bfloat16)

    @pl.when((h == 1) & (p == 0))
    def _():
        for n in range(STRIPS):
            @functools.partial(loop, chunks)
            def _(i):
                row = local_row(i)
                gain = aux_ref[pl.ds(row // BLOCK, 1), :][:, n * strip:(n + 1) * strip]
                value = 1.0 + w_ref[pl.ds(row, ROWS), columns(n)].astype(jnp.float32) * gain
                right[pl.ds(row, ROWS), columns(n)] = value
                trail[pl.ds(row, ROWS), columns(n)] = value.astype(jnp.bfloat16)
            b_copy(n).start()

    def wait_info(k):
        sender = (me + total - k) % total
        pltpu.make_async_remote_copy(
            src_ref=info, dst_ref=infos.at[sender], send_sem=info_send.at[k], recv_sem=info_recv.at[k],
            device_id=(base + sender // parts, sender % parts), device_id_type=MESH).wait_recv()

    for k in range(1, total):
        wait_info(k)
        info_copy(k).wait_send()

    def emission(m, part):
        return infos[m * parts + part, 0:1, :]

    def peak(m):
        top = emission(m, 0)
        for part in range(1, parts):
            top = jnp.maximum(top, emission(m, part))
        return jnp.max(top, axis=1, keepdims=True)

    left_peak = jnp.where(p == 0, peak(0), peak(2))
    weights = [
        jnp.exp(jnp.where(p == 0, emission(0, part), emission(2, part)) - left_peak) for part in range(parts)
    ]
    middle_peak = peak(1)
    middle_emission = infos[parts + s, 0:1, :]
    middle_scale = jnp.exp(middle_emission - middle_peak) * 2.0 ** LEAD_SHIFT

    def product(row, count, n):
        acc = None
        for part in range(parts):
            lead = (left[part, pl.ds(row, count), :] * weights[part]).astype(jnp.bfloat16)
            block = slice(part * width, (part + 1) * width)
            right_block = trail[block, :] if n is None else trail[block, n * strip:(n + 1) * strip]
            term = jnp.dot(lead, right_block, preferred_element_type=jnp.float32)
            acc = term if acc is None else acc + term
        return acc

    def take(i, row):
        x_copy(i, row).wait_recv()
        y_copy(0, i, row, s, core).start()
        y_copy(1, i, row, s, over).start()

    def relay(i, row):
        y_copy(1, i, row, over, over).wait_recv()
        y_copy(2, i, row, over, core).start()

    def have(i, row):
        y_copy(0, i, row, core, core).wait_recv()
        y_copy(2, i, row, far, core).wait_recv()

    @pl.when((p == 1) & (h == 1))
    def _():
        @functools.partial(loop, chunks + 2)
        def _(t):
            @pl.when(t < chunks)
            def _():
                take(t, rows_of(t))

            @pl.when((t >= 1) & (t < chunks + 1))
            def _():
                relay(t - 1, rows_of(t - 1))

            @pl.when((t >= 3) & (t % 2 == 1))
            def _():
                i = t - 3
                row = pl.multiple_of(rows_of(i), 2 * ROWS)
                have(i, rows_of(i))
                have(i + 1, rows_of(i + 1))
                pair[pl.ds(row, 2 * ROWS), :] = product(row, 2 * ROWS, None) * 2.0 ** TRAIL_SHIFT
                pair_copy(1, i, device(1, 0, s)).start()
                pair_copy(0, i, device(0, 1, s)).start()
                pair_copy(1, i + 1, device(1, 0, s)).start()
                pair_copy(0, i + 1, device(0, 1, s)).start()

        @functools.partial(loop, per_quarter)
        def _(g):
            q_copy(g).wait_recv()
            g_copy(0, g, s, core).start()
            v_copy(g).wait_recv()
            g_copy(2, g, over, core).start()

    @pl.when((p == 0) & (h == 1))
    def _():
        @functools.partial(loop, half + 5)
        def _(t):
            @pl.when(t < half)
            def _():
                take(t, half_rows(t, 1))

            @pl.when((t >= 1) & (t < half + 1))
            def _():
                relay(t - 1, half_rows(t - 1, 1))

            @pl.when((t >= 2) & (t < half + 2))
            def _():
                i = t - 2
                g = i // 2
                row = half_rows(i, 1)
                have(i, row)
                value = product(row, ROWS, None) * middle_scale

                @pl.when(i % 2 == 0)
                def _():
                    stage[pl.ds(local_row(g), ROWS), :] = value
                    w_copy(g).start()
                    q_copy(g).start()

                @pl.when(i % 2 == 1)
                def _():
                    first[s, pl.ds(local_row(g), ROWS), :] = value
                    g_copy(1, g, s, over).start()
                    g_copy(0, g, s, core).start()

            @pl.when(t >= 5)
            def _():
                i = t - 5
                g = i // 2

                @pl.when(i % 2 == 0)
                def _():
                    w_copy(g).wait_recv()
                    v_copy(g).start()

                @pl.when(i % 2 == 1)
                def _():
                    g_copy(1, g, over, over).wait_recv()
                    g_copy(2, g, over, core).start()

    def strip_out(n):
        g_strip(1, n, s, over).start()
        g_strip(0, n, s, core).start()

    def strip_relay(n):
        g_strip(1, n, over, over).wait_recv()
        g_strip(2, n, over, core).start()

    @pl.when((p == 1) & (h == 0))
    def _():
        for low, high, arrive, pass_on in SCHEDULE:
            def relay_pair(i, c):
                pair_copy(0, i, device(0, 0, s)).wait_recv()
                pair_copy(0, i, device(0, 0, s)).start()
                return c
            lax.fori_loop(chunks * low // 32, chunks * high // 32, relay_pair, 0)
            if arrive is not None:
                q_strip(arrive).wait_recv()
                strip_out(arrive)
            if pass_on is not None:
                strip_relay(pass_on)

    @pl.when((p == 0) & (h == 0))
    def _():
        @functools.partial(loop, half)
        def _(i):
            relay(i, half_rows(i, 0))

        @functools.partial(loop, half)
        def _(i):
            have(i, half_rows(i, 0))

        for n in range(STRIPS):
            b_copy(n).wait_recv()

            @functools.partial(loop, chunks)
            def _(i):
                row = local_row(i)
                trail[pl.ds(row, ROWS), columns(n)] = right[pl.ds(row, ROWS), columns(n)].astype(jnp.bfloat16)

            scale = middle_scale[:, n * strip:(n + 1) * strip]

            @functools.partial(loop, quarter_rows // TILE)
            def _(j):
                row = pl.multiple_of(j * TILE, TILE)
                source = pl.multiple_of(2 * quarter_rows + j * TILE, TILE)
                stage[pl.ds(row, TILE), columns(n)] = product(source, TILE, n) * scale

            q_strip(n).start()

            @functools.partial(loop, quarter_rows // TILE)
            def _(j):
                row = pl.multiple_of(j * TILE, TILE)
                first[s, pl.ds(row, TILE), columns(n)] = product(row, TILE, n) * scale

            strip_out(n)
            if n > 0:
                strip_relay(n - 1)
        strip_relay(STRIPS - 1)

    @pl.when(p == 0)
    def _():
        @functools.partial(loop, chunks)
        def _(i):
            pair_copy(0, i, device(1, h, s)).wait_recv()

    def to_trail(i, c):
        row = pl.multiple_of(i * ROWS, ROWS)
        trail[pl.ds(row, ROWS), :] = pair[pl.ds(row, ROWS), :].astype(jnp.bfloat16)
        return c

    lax.fori_loop(0, chunks, to_trail, 0)

    @pl.when(h == 1)
    def _():
        @functools.partial(loop, per_quarter)
        def _(g):
            g_copy(0, g, core, core).wait_recv()
            g_copy(2, g, far, core).wait_recv()

    @pl.when(h == 0)
    def _():
        for n in range(STRIPS):
            g_strip(0, n, core, core).wait_recv()
            g_strip(2, n, far, core).wait_recv()

    log_shares = infos[0, 1:2, :] + infos[parts, 1:2, :] + infos[2 * parts, 1:2, :] + infos[3 * parts, 1:2, :]
    shift = math.log(2.0) * (LEAD_SHIFT + TRAIL_SHIFT)
    last_emission = jnp.zeros_like(middle_emission)
    for part in range(parts):
        last_emission = jnp.where(s == part, emission(3, part), last_emission)
    offset = last_emission + log_shares + (peak(0) + middle_peak + peak(2) - shift)

    out_rows = out_ref.shape[0]
    tile = 128

    def finish(i, c):
        row = pl.multiple_of(i * tile, tile)
        acc = None
        for part in range(parts):
            term = jnp.dot(
                first[part, pl.ds(row, tile), :].astype(jnp.bfloat16), trail[part * width:(part + 1) * width, :],
                preferred_element_type=jnp.float32)
            acc = term if acc is None else acc + term
        out_ref[pl.ds(row, tile), :] = jnp.log(acc) + offset
        return c

    lax.fori_loop(0, out_rows // tile, finish, 0)

    def drain_left(i, row):
        y_copy(0, i, row, s, core).wait_send()
        y_copy(1, i, row, s, over).wait_send()
        y_copy(2, i, row, over, core).wait_send()

    @pl.when((p == 1) & (h == 1))
    def _():
        @functools.partial(loop, chunks)
        def _(i):
            drain_left(i, rows_of(i))
            pair_copy(0, i, device(0, 1, s)).wait_send()
            pair_copy(1, i, device(1, 0, s)).wait_send()

        @functools.partial(loop, per_quarter)
        def _(g):
            g_copy(0, g, s, core).wait_send()
            g_copy(2, g, over, core).wait_send()

    @pl.when((p == 1) & (h == 0))
    def _():
        @functools.partial(loop, chunks)
        def _(i):
            x_copy(i, rows_of(i)).wait_send()
            pair_copy(0, i, device(0, 0, s)).wait_send()

    @pl.when((p == 0) & (h == 1))
    def _():
        for n in range(STRIPS):
            b_copy(n).wait_send()

        @functools.partial(loop, half)
        def _(i):
            drain_left(i, half_rows(i, 1))

        @functools.partial(loop, per_quarter)
        def _(g):
            q_copy(g).wait_send()
            w_copy(g).wait_send()
            v_copy(g).wait_send()
            g_copy(0, g, s, core).wait_send()
            g_copy(1, g, s, over).wait_send()
            g_copy(2, g, over, core).wait_send()

    @pl.when((p == 0) & (h == 0))
    def _():
        @functools.partial(loop, half)
        def _(i):
            x_copy(i, half_rows(i, 1)).wait_send()
            drain_left(i, half_rows(i, 0))

        for n in range(STRIPS):
            q_strip(n).wait_send()

    @pl.when(h == 0)
    def _():
        for n in range(STRIPS):
            g_strip(0, n, s, core).wait_send()
            g_strip(1, n, s, over).wait_send()
            g_strip(2, n, over, core).wait_send()


def on_device(parts, trans_weight, pattern, boundary, log_emit):
    weight = trans_weight[0]
    states, width = weight.shape
    blocks = pattern.shape[0]
    restart = 0.0001 + 0.4999 * boundary.astype(jnp.float32)
    first_block = lax.axis_index("state") * (width // BLOCK)
    mine = lax.dynamic_slice_in_dim(pattern, first_block, width // BLOCK, 1).astype(jnp.float32)
    gain = jnp.repeat(mine, BLOCK, axis=1) * (4.0 * (1.0 - restart) / restart)
    share = jnp.broadcast_to(jnp.log(restart / states)[:, None], (7, width))
    aux = jnp.concatenate([gain, log_emit, share], axis=0)
    chunks = states // ROWS
    dma = pltpu.SemaphoreType.DMA
    vmem = pl.BlockSpec(memory_space=pltpu.VMEM)
    return pl.pallas_call(
        functools.partial(kernel, parts),
        out_shape=jax.ShapeDtypeStruct((states // 4, width), jnp.float32),
        in_specs=[vmem, vmem],
        out_specs=vmem,
        scratch_shapes=[
            pltpu.VMEM((parts, states, width), jnp.float32),
            pltpu.VMEM((states, width), jnp.bfloat16),
            pltpu.VMEM((states, width), jnp.float32),
            pltpu.VMEM((parts, states // 4, width), jnp.float32),
            pltpu.VMEM((states, width), jnp.float32),
            pltpu.VMEM((states, width), jnp.float32),
            pltpu.VMEM((4 * parts, 8, width), jnp.float32),
            dma((4 * parts,)), dma((4 * parts,)),
            dma((chunks,)), dma((chunks,)),
            dma((3, chunks)), dma((3, chunks)),
            dma((2, chunks)), dma((chunks,)),
            dma((chunks // 4,)), dma((chunks // 4,)),
            dma((3, chunks // 4)), dma((3, chunks // 4)),
            dma((STRIPS,)), dma((STRIPS,)),
            dma((chunks // 4,)), dma((chunks // 4,)), dma((chunks // 4,)), dma((chunks // 4,)),
        ],
        compiler_params=pltpu.CompilerParams(
            collective_id=0, has_side_effects=True, vmem_limit_bytes=52 * 1024 * 1024
        ),
    )(weight, aux)


def solution(mesh):
    return jax.shard_map(
        functools.partial(on_device, mesh.shape["state"]),
        mesh=mesh,
        in_specs=(P("tm", None, "state"), P(), P("tm"), P("tm", "state")),
        out_specs=P("tm", "state"),
        check_vma=False,
    )
```

```python
import functools
import math

import jax
import jax.numpy as jnp
from jax import lax
from jax.experimental import pallas as pl
from jax.experimental.pallas import tpu as pltpu
from jax.sharding import PartitionSpec as P

BLOCK = 128
ROWS = 64
STRIPS = 4
TILE = 256
SCHEDULE = (
    (0, 16, 0, None), (16, 19, None, 0), (19, 21, 1, None), (21, 24, None, 1), (24, 26, 2, None), (26, 30, None, 2),
    (30, 32, 3, 3),
)
LEAD_SHIFT = 12
TRAIL_SHIFT = -49
MESH = pl.DeviceIdType.MESH


def kernel(
    parts, w_ref, aux_ref, out_ref, left, trail, pair, first, stage, right, infos,
    info_send, info_recv, x_send, x_recv, y_send, y_recv, p_send, p_recv,
    q_send, q_recv, g_send, g_recv, b_send, b_recv, w_send, w_recv, v_send, v_recv,
):
    states, width = w_ref.shape
    blocks = states // BLOCK
    chunks = states // ROWS
    per_quarter = chunks // 4
    half = chunks // 2
    quarter_rows = states // 4
    strip = width // STRIPS
    tm = lax.axis_index("tm")
    s = lax.axis_index("state")
    base = tm // 4 * 4
    member = tm % 4
    p = member // 2
    h = member % 2
    me = member * parts + s
    core = s + 1 - 2 * (s % 2)
    over = (s + 2) % 4
    far = (core + 2) % 4
    total = 4 * parts

    def device(p_, h_, s_):
        return (base + 2 * p_ + h_, s_)

    barrier = pltpu.get_barrier_semaphore()
    for k in range(1, total):
        peer = (me + k) % total
        pl.semaphore_signal(barrier, inc=1, device_id=(base + peer // parts, peer % parts), device_id_type=MESH)
    pl.semaphore_wait(barrier, total - 1)

    info = aux_ref.at[pl.ds(blocks, 8)]

    def info_copy(k):
        peer = (me + k) % total
        return pltpu.make_async_remote_copy(
            src_ref=info, dst_ref=infos.at[me], send_sem=info_send.at[k], recv_sem=info_recv.at[k],
            device_id=(base + peer // parts, peer % parts), device_id_type=MESH)

    for k in range(1, total):
        info_copy(k).start()
    infos[me] = aux_ref[blocks:blocks + 8, :]

    def rows_of(i):
        return pl.multiple_of(i * ROWS, ROWS)

    def remote(ref, slot, row, send, recv, target):
        view = ref.at[slot, pl.ds(row, ROWS)] if slot is not None else ref.at[pl.ds(row, ROWS)]
        return pltpu.make_async_remote_copy(
            src_ref=view, dst_ref=view, send_sem=send, recv_sem=recv, device_id=target, device_id_type=MESH)

    def half_rows(i, side):
        return pl.multiple_of(((2 + side - 2 * (i % 2)) * per_quarter + i // 2) * ROWS, ROWS)

    def x_copy(i, row):
        return remote(left, s, row, x_send.at[i], x_recv.at[i], device(p, 1 - h, s))

    def y_copy(kind, i, row, slot, target):
        return remote(left, slot, row, y_send.at[kind, i], y_recv.at[kind, i], device(p, h, target))

    def pair_copy(kind, i, target):
        return remote(pair, None, rows_of(i), p_send.at[kind, i], p_recv.at[i], target)

    def local_row(g):
        return pl.multiple_of(g * ROWS, ROWS)

    def g_copy(kind, g, slot, target):
        return remote(first, slot, local_row(g), g_send.at[kind, g], g_recv.at[kind, g], device(p, h, target))

    def columns(n):
        return pl.ds(n * strip, strip)

    def g_strip(kind, n, slot, target):
        view = first.at[slot, :, columns(n)]
        return pltpu.make_async_remote_copy(
            src_ref=view, dst_ref=view, send_sem=g_send.at[kind, n], recv_sem=g_recv.at[kind, n],
            device_id=device(p, h, target), device_id_type=MESH)

    def q_copy(g):
        return pltpu.make_async_remote_copy(
            src_ref=stage.at[pl.ds(local_row(g), ROWS)], dst_ref=first.at[s, pl.ds(local_row(g), ROWS)],
            send_sem=q_send.at[g], recv_sem=q_recv.at[g], device_id=device(1 - p, 1, s), device_id_type=MESH)

    def q_strip(n):
        return pltpu.make_async_remote_copy(
            src_ref=stage.at[pl.ds(0, quarter_rows), columns(n)], dst_ref=first.at[s, :, columns(n)],
            send_sem=q_send.at[n], recv_sem=q_recv.at[n], device_id=device(1 - p, 0, s), device_id_type=MESH)

    def w_copy(g):
        return pltpu.make_async_remote_copy(
            src_ref=stage.at[pl.ds(local_row(g), ROWS)], dst_ref=stage.at[pl.ds(local_row(g + per_quarter), ROWS)],
            send_sem=w_send.at[g], recv_sem=w_recv.at[g], device_id=device(p, h, over), device_id_type=MESH)

    def v_copy(g):
        return pltpu.make_async_remote_copy(
            src_ref=stage.at[pl.ds(local_row(g + per_quarter), ROWS)], dst_ref=first.at[over, pl.ds(local_row(g), ROWS)],
            send_sem=v_send.at[g], recv_sem=v_recv.at[g], device_id=device(1 - p, 1, s), device_id_type=MESH)

    def b_copy(n):
        view = right.at[:, columns(n)]
        return pltpu.make_async_remote_copy(
            src_ref=view, dst_ref=view, send_sem=b_send.at[n], recv_sem=b_recv.at[n],
            device_id=device(p, 1 - h, s), device_id_type=MESH)

    def odds(row):
        gain = aux_ref[pl.ds(row // BLOCK, 1), :]
        return 1.0 + w_ref[pl.ds(row, ROWS), :].astype(jnp.float32) * gain

    def loop(count, body):
        def run(i, c):
            body(i)
            return c
        lax.fori_loop(0, count, run, 0)

    @pl.when((h == 0) & (p == 1))
    def _():
        @functools.partial(loop, chunks)
        def _(i):
            row = rows_of(i)
            left[s, pl.ds(row, ROWS), :] = odds(row)
            x_copy(i, row).start()

    @pl.when((h == 0) & (p == 0))
    def _():
        @functools.partial(loop, half)
        def _(i):
            row = half_rows(i, 1)
            left[s, pl.ds(row, ROWS), :] = odds(row)
            x_copy(i, row).start()
            near = half_rows(i, 0)
            left[s, pl.ds(near, ROWS), :] = odds(near)
            y_copy(0, i, near, s, core).start()
            y_copy(1, i, near, s, over).start()

    @pl.when((h == 1) & (p == 1))
    def _():
        @functools.partial(loop, chunks)
        def _(i):
            row = local_row(i)
            trail[pl.ds(row, ROWS), :] = odds(row).astype(jnp.bfloat16)

    @pl.when((h == 1) & (p == 0))
    def _():
        for n in range(STRIPS):
            @functools.partial(loop, chunks)
            def _(i):
                row = local_row(i)
                gain = aux_ref[pl.ds(row // BLOCK, 1), :][:, n * strip:(n + 1) * strip]
                value = 1.0 + w_ref[pl.ds(row, ROWS), columns(n)].astype(jnp.float32) * gain
                right[pl.ds(row, ROWS), columns(n)] = value
                trail[pl.ds(row, ROWS), columns(n)] = value.astype(jnp.bfloat16)
            b_copy(n).start()

    def wait_info(k):
        sender = (me + total - k) % total
        pltpu.make_async_remote_copy(
            src_ref=info, dst_ref=infos.at[sender], send_sem=info_send.at[k], recv_sem=info_recv.at[k],
            device_id=(base + sender // parts, sender % parts), device_id_type=MESH).wait_recv()

    for k in range(1, total):
        wait_info(k)
        info_copy(k).wait_send()

    def emission(m, part):
        return infos[m * parts + part, 0:1, :]

    def peak(m):
        top = emission(m, 0)
        for part in range(1, parts):
            top = jnp.maximum(top, emission(m, part))
        return jnp.max(top, axis=1, keepdims=True)

    left_peak = jnp.where(p == 0, peak(0), peak(2))
    weights = [
        jnp.exp(jnp.where(p == 0, emission(0, part), emission(2, part)) - left_peak) for part in range(parts)
    ]
    middle_peak = peak(1)
    middle_emission = infos[parts + s, 0:1, :]
    middle_scale = jnp.exp(middle_emission - middle_peak) * 2.0 ** LEAD_SHIFT

    def product(row, count, n):
        acc = None
        for part in range(parts):
            lead = (left[part, pl.ds(row, count), :] * weights[part]).astype(jnp.bfloat16)
            block = slice(part * width, (part + 1) * width)
            right_block = trail[block, :] if n is None else trail[block, n * strip:(n + 1) * strip]
            term = jnp.dot(lead, right_block, preferred_element_type=jnp.float32)
            acc = term if acc is None else acc + term
        return acc

    def take(i, row):
        x_copy(i, row).wait_recv()
        y_copy(0, i, row, s, core).start()
        y_copy(1, i, row, s, over).start()

    def relay(i, row):
        y_copy(1, i, row, over, over).wait_recv()
        y_copy(2, i, row, over, core).start()

    def have(i, row):
        y_copy(0, i, row, core, core).wait_recv()
        y_copy(2, i, row, far, core).wait_recv()

    @pl.when((p == 1) & (h == 1))
    def _():
        @functools.partial(loop, chunks + 2)
        def _(t):
            @pl.when(t < chunks)
            def _():
                take(t, rows_of(t))

            @pl.when((t >= 1) & (t < chunks + 1))
            def _():
                relay(t - 1, rows_of(t - 1))

            @pl.when(t >= 2)
            def _():
                i = t - 2
                row = rows_of(i)
                have(i, row)
                pair[pl.ds(row, ROWS), :] = product(row, ROWS, None) * 2.0 ** TRAIL_SHIFT
                pair_copy(1, i, device(1, 0, s)).start()
                pair_copy(0, i, device(0, 1, s)).start()

        @functools.partial(loop, per_quarter)
        def _(g):
            q_copy(g).wait_recv()
            g_copy(0, g, s, core).start()
            v_copy(g).wait_recv()
            g_copy(2, g, over, core).start()

    @pl.when((p == 0) & (h == 1))
    def _():
        @functools.partial(loop, half + 5)
        def _(t):
            @pl.when(t < half)
            def _():
                take(t, half_rows(t, 1))

            @pl.when((t >= 1) & (t < half + 1))
            def _():
                relay(t - 1, half_rows(t - 1, 1))

            @pl.when((t >= 2) & (t < half + 2))
            def _():
                i = t - 2
                g = i // 2
                row = half_rows(i, 1)
                have(i, row)
                value = product(row, ROWS, None) * middle_scale

                @pl.when(i % 2 == 0)
                def _():
                    stage[pl.ds(local_row(g), ROWS), :] = value
                    w_copy(g).start()
                    q_copy(g).start()

                @pl.when(i % 2 == 1)
                def _():
                    first[s, pl.ds(local_row(g), ROWS), :] = value
                    g_copy(1, g, s, over).start()
                    g_copy(0, g, s, core).start()

            @pl.when(t >= 5)
            def _():
                i = t - 5
                g = i // 2

                @pl.when(i % 2 == 0)
                def _():
                    w_copy(g).wait_recv()
                    v_copy(g).start()

                @pl.when(i % 2 == 1)
                def _():
                    g_copy(1, g, over, over).wait_recv()
                    g_copy(2, g, over, core).start()

    def strip_out(n):
        g_strip(1, n, s, over).start()
        g_strip(0, n, s, core).start()

    def strip_relay(n):
        g_strip(1, n, over, over).wait_recv()
        g_strip(2, n, over, core).start()

    @pl.when((p == 1) & (h == 0))
    def _():
        for low, high, arrive, pass_on in SCHEDULE:
            def relay_pair(i, c):
                pair_copy(0, i, device(0, 0, s)).wait_recv()
                pair_copy(0, i, device(0, 0, s)).start()
                return c
            lax.fori_loop(chunks * low // 32, chunks * high // 32, relay_pair, 0)
            if arrive is not None:
                q_strip(arrive).wait_recv()
                strip_out(arrive)
            if pass_on is not None:
                strip_relay(pass_on)

    @pl.when((p == 0) & (h == 0))
    def _():
        @functools.partial(loop, half)
        def _(i):
            relay(i, half_rows(i, 0))

        @functools.partial(loop, half)
        def _(i):
            have(i, half_rows(i, 0))

        for n in range(STRIPS):
            b_copy(n).wait_recv()

            @functools.partial(loop, chunks)
            def _(i):
                row = local_row(i)
                trail[pl.ds(row, ROWS), columns(n)] = right[pl.ds(row, ROWS), columns(n)].astype(jnp.bfloat16)

            scale = middle_scale[:, n * strip:(n + 1) * strip]

            @functools.partial(loop, quarter_rows // TILE)
            def _(j):
                row = pl.multiple_of(j * TILE, TILE)
                source = pl.multiple_of(2 * quarter_rows + j * TILE, TILE)
                stage[pl.ds(row, TILE), columns(n)] = product(source, TILE, n) * scale

            q_strip(n).start()

            @functools.partial(loop, quarter_rows // TILE)
            def _(j):
                row = pl.multiple_of(j * TILE, TILE)
                first[s, pl.ds(row, TILE), columns(n)] = product(row, TILE, n) * scale

            strip_out(n)
            if n > 0:
                strip_relay(n - 1)
        strip_relay(STRIPS - 1)

    @pl.when(p == 0)
    def _():
        @functools.partial(loop, chunks)
        def _(i):
            pair_copy(0, i, device(1, h, s)).wait_recv()

    def to_trail(i, c):
        row = pl.multiple_of(i * ROWS, ROWS)
        trail[pl.ds(row, ROWS), :] = pair[pl.ds(row, ROWS), :].astype(jnp.bfloat16)
        return c

    lax.fori_loop(0, chunks, to_trail, 0)

    @pl.when(h == 1)
    def _():
        @functools.partial(loop, per_quarter)
        def _(g):
            g_copy(0, g, core, core).wait_recv()
            g_copy(2, g, far, core).wait_recv()

    @pl.when(h == 0)
    def _():
        for n in range(STRIPS):
            g_strip(0, n, core, core).wait_recv()
            g_strip(2, n, far, core).wait_recv()

    log_shares = infos[0, 1:2, :] + infos[parts, 1:2, :] + infos[2 * parts, 1:2, :] + infos[3 * parts, 1:2, :]
    shift = math.log(2.0) * (LEAD_SHIFT + TRAIL_SHIFT)
    last_emission = jnp.zeros_like(middle_emission)
    for part in range(parts):
        last_emission = jnp.where(s == part, emission(3, part), last_emission)
    offset = last_emission + log_shares + (peak(0) + middle_peak + peak(2) - shift)

    out_rows = out_ref.shape[0]
    tile = 128

    def finish(i, c):
        row = pl.multiple_of(i * tile, tile)
        acc = None
        for part in range(parts):
            term = jnp.dot(
                first[part, pl.ds(row, tile), :].astype(jnp.bfloat16), trail[part * width:(part + 1) * width, :],
                preferred_element_type=jnp.float32)
            acc = term if acc is None else acc + term
        out_ref[pl.ds(row, tile), :] = jnp.log(acc) + offset
        return c

    lax.fori_loop(0, out_rows // tile, finish, 0)

    def drain_left(i, row):
        y_copy(0, i, row, s, core).wait_send()
        y_copy(1, i, row, s, over).wait_send()
        y_copy(2, i, row, over, core).wait_send()

    @pl.when((p == 1) & (h == 1))
    def _():
        @functools.partial(loop, chunks)
        def _(i):
            drain_left(i, rows_of(i))
            pair_copy(0, i, device(0, 1, s)).wait_send()
            pair_copy(1, i, device(1, 0, s)).wait_send()

        @functools.partial(loop, per_quarter)
        def _(g):
            g_copy(0, g, s, core).wait_send()
            g_copy(2, g, over, core).wait_send()

    @pl.when((p == 1) & (h == 0))
    def _():
        @functools.partial(loop, chunks)
        def _(i):
            x_copy(i, rows_of(i)).wait_send()
            pair_copy(0, i, device(0, 0, s)).wait_send()

    @pl.when((p == 0) & (h == 1))
    def _():
        for n in range(STRIPS):
            b_copy(n).wait_send()

        @functools.partial(loop, half)
        def _(i):
            drain_left(i, half_rows(i, 1))

        @functools.partial(loop, per_quarter)
        def _(g):
            q_copy(g).wait_send()
            w_copy(g).wait_send()
            v_copy(g).wait_send()
            g_copy(0, g, s, core).wait_send()
            g_copy(1, g, s, over).wait_send()
            g_copy(2, g, over, core).wait_send()

    @pl.when((p == 0) & (h == 0))
    def _():
        @functools.partial(loop, half)
        def _(i):
            x_copy(i, half_rows(i, 1)).wait_send()
            drain_left(i, half_rows(i, 0))

        for n in range(STRIPS):
            q_strip(n).wait_send()

    @pl.when(h == 0)
    def _():
        for n in range(STRIPS):
            g_strip(0, n, s, core).wait_send()
            g_strip(1, n, s, over).wait_send()
            g_strip(2, n, over, core).wait_send()


def on_device(parts, trans_weight, pattern, boundary, log_emit):
    weight = trans_weight[0]
    states, width = weight.shape
    blocks = pattern.shape[0]
    restart = 0.0001 + 0.4999 * boundary.astype(jnp.float32)
    first_block = lax.axis_index("state") * (width // BLOCK)
    mine = lax.dynamic_slice_in_dim(pattern, first_block, width // BLOCK, 1).astype(jnp.float32)
    gain = jnp.repeat(mine, BLOCK, axis=1) * (4.0 * (1.0 - restart) / restart)
    share = jnp.broadcast_to(jnp.log(restart / states)[:, None], (7, width))
    aux = jnp.concatenate([gain, log_emit, share], axis=0)
    chunks = states // ROWS
    dma = pltpu.SemaphoreType.DMA
    vmem = pl.BlockSpec(memory_space=pltpu.VMEM)
    return pl.pallas_call(
        functools.partial(kernel, parts),
        out_shape=jax.ShapeDtypeStruct((states // 4, width), jnp.float32),
        in_specs=[vmem, vmem],
        out_specs=vmem,
        scratch_shapes=[
            pltpu.VMEM((parts, states, width), jnp.float32),
            pltpu.VMEM((states, width), jnp.bfloat16),
            pltpu.VMEM((states, width), jnp.float32),
            pltpu.VMEM((parts, states // 4, width), jnp.float32),
            pltpu.VMEM((states, width), jnp.float32),
            pltpu.VMEM((states, width), jnp.float32),
            pltpu.VMEM((4 * parts, 8, width), jnp.float32),
            dma((4 * parts,)), dma((4 * parts,)),
            dma((chunks,)), dma((chunks,)),
            dma((3, chunks)), dma((3, chunks)),
            dma((2, chunks)), dma((chunks,)),
            dma((chunks // 4,)), dma((chunks // 4,)),
            dma((3, chunks // 4)), dma((3, chunks // 4)),
            dma((STRIPS,)), dma((STRIPS,)),
            dma((chunks // 4,)), dma((chunks // 4,)), dma((chunks // 4,)), dma((chunks // 4,)),
        ],
        compiler_params=pltpu.CompilerParams(
            collective_id=0, has_side_effects=True, vmem_limit_bytes=52 * 1024 * 1024
        ),
    )(weight, aux)


def solution(mesh):
    return jax.shard_map(
        functools.partial(on_device, mesh.shape["state"]),
        mesh=mesh,
        in_specs=(P("tm", None, "state"), P(), P("tm"), P("tm", "state")),
        out_specs=P("tm", "state"),
        check_vma=False,
    )
```
